512 devices in a mesh: aa: 32 (over z, core), ba: 16 (over x, y).
Axes of the slice: x: 4, y: 4, z: 16, core: 2. Of those that a mesh axis runs over, the one named last changes fastest.
Arguments:
- right_sides: bfloat16 [524288, 512], P(('aa', 'ba')), may hold values from -6 to 6
- point_order: int32 [512, 1024], P(('aa', 'ba')), may hold values from 0 to 1023, each once within a row
- skeleton: int32 [512, 128], P(('aa', 'ba')), may hold values from 0 to 1023, as said below
- leaf_inverse: bfloat16 [524288, 1024], P(('aa', 'ba')), may hold values from -1 to 3.5
- leaf_basis: bfloat16 [524288, 128], P(('aa', 'ba')), may hold values from -0.1875 to 0.1875
- group_core: bfloat16 [65536, 2048], P(('aa', 'ba')), may hold values from -1 to 2, as said below
- transfer: float32 [65536, 128], P(('aa', 'ba')), may hold values from -0.5 to 0.5
- top_core: bfloat16 [4096, 4096], P(('aa', 'ba')), may hold values from -1 to 2
Outputs:
- solution: bfloat16 [524288, 512], P(('aa', 'ba'))
The draws below stay inside these ranges and needn't reach their ends.
Inputs may be any that keep to these rules, and one draw needn't show every extreme that they name: `skeleton`: each row holds 128 different indices in increasing order. `group_core`: each group's block of 2048 rows is symmetric.
All inputs are finite; a program needn't handle non-finite values.
Results may differ from the reference program's by a relative error of at most 0.014.
Values may be sent and summed in bfloat16 or wider, within the bound.
A program may use at most 64 MiB of HBM per device.

```python
import math
import jax
import jax.numpy as jnp
from jax import lax

LEAF = 1024
RANK = 128
RHS = 512
LEAVES = 512
POINTS = 524288
GROUP = 2048
TOP = 4096
N_AA = 32
N_BA = 16


def draw_skeleton(key, part):
    leaf_keys = jax.random.split(key, LEAVES)
    shuffled = jax.vmap(lambda leaf_key: jax.random.permutation(leaf_key, LEAF))(leaf_keys)
    return jnp.sort(shuffled[:, :RANK], axis=1).astype(jnp.int32)


def draw_leaf_inverse(key, part):
    diag_key, off_key = jax.random.split(jax.random.fold_in(key, 11))
    diagonal = jnp.exp(jax.random.uniform(diag_key, (LEAVES, LEAF), jnp.float32, math.log(0.5), math.log(2.0)))
    spread = jax.random.truncated_normal(off_key, -4.0, 4.0, (LEAVES, LEAF, LEAF), jnp.float32) * (0.5 / math.sqrt(LEAF))
    position = jnp.arange(LEAF)
    matrix = spread.at[:, position, position].add(diagonal)
    return matrix.reshape(LEAVES * LEAF, LEAF).astype(jnp.bfloat16)


def core_matrix(key, groups, order, scale):
    diag_key, off_key = jax.random.split(key)
    diagonal = jnp.exp(jax.random.uniform(diag_key, (groups, order), jnp.float32, math.log(0.3), 0.0))
    spread = jax.random.truncated_normal(off_key, -4.0, 4.0, (groups, order, order), jnp.float32)
    matrix = (spread + jnp.swapaxes(spread, 1, 2)) * (0.6 / math.sqrt(2.0 * order))
    position = jnp.arange(order)
    matrix = matrix.at[:, position, position].add(diagonal)
    return matrix * scale


def draw_group_core(key, part):
    matrix = core_matrix(jax.random.fold_in(key, 23), TOP // RANK, GROUP, 1.0)
    return matrix.reshape(TOP // RANK * GROUP, GROUP).astype(jnp.bfloat16)


def draw_top_core(key, part):
    matrix = core_matrix(jax.random.fold_in(key, 37), 1, TOP, 1.0 / math.sqrt(GROUP // RANK))
    return matrix.reshape(TOP, TOP).astype(jnp.bfloat16)


def block_scale(own_key, shape, cuts, low, high):
    def one(axis_at, shards_of):
        draws = jax.random.uniform(jax.random.fold_in(jax.random.fold_in(own_key, 6), axis_at), (shards_of,), jnp.float32, low / len(cuts), high / len(cuts))
        return jnp.repeat(jnp.exp(draws), shape[axis_at] // shards_of).reshape((-1,) + (1,) * (len(shape) - axis_at - 1))

    factor_of = one(*cuts[0])
    for cut in cuts[1:]:
        factor_of = factor_of * one(*cut)
    return factor_of


def gaussian(own_key, dims, deviation, bound, pieces=(), kind=jnp.bfloat16):
    array = deviation * jax.random.normal(own_key, dims, jnp.float32)
    if pieces:
        array = array * block_scale(own_key, dims, pieces, -0.22, 0.18)
    return jnp.clip(array, -bound, bound).astype(kind)


def setup_inputs(seed: int = 0) -> dict:
    key_list = jax.random.split(jax.random.key(seed), 9)
    right_sides = gaussian(key_list[0], (POINTS, RHS), 1.0, 6.0, ((0, 512),))
    point_order = jax.vmap(lambda own: jax.random.permutation(own, LEAF))(jax.random.split(key_list[1], LEAVES)).reshape((LEAVES, LEAF)).astype(jnp.int32)
    skeleton = draw_skeleton(jax.random.fold_in(key_list[8], 71), 0)
    leaf_inverse = draw_leaf_inverse(jax.random.fold_in(key_list[8], 71), 0)
    leaf_basis = gaussian(key_list[4], (POINTS, RANK), LEAF ** -0.5, 0.1875, ((0, 512),))
    group_core = draw_group_core(jax.random.fold_in(key_list[8], 71), 0)
    transfer = gaussian(key_list[6], (LEAVES * RANK, RANK), RANK ** -0.5, 0.5, ((0, 512),), jnp.float32)
    top_core = draw_top_core(jax.random.fold_in(key_list[8], 71), 0)
    return {"right_sides": right_sides, "point_order": point_order, "skeleton": skeleton, "leaf_inverse": leaf_inverse, "leaf_basis": leaf_basis, "group_core": group_core, "transfer": transfer, "top_core": top_core}


def rounded(values):
    return lax.optimization_barrier(values.astype(jnp.bfloat16)).astype(jnp.float32)


def leaf_up(leaf_args):
    sides, ordering, skel_rows, inverse, leaf_base = leaf_args
    ordered = sides[ordering].astype(jnp.float32)
    applied = jnp.dot(inverse.astype(jnp.float32), ordered)
    coeffs = jnp.dot(leaf_base.astype(jnp.float32).T, rounded(applied)) + applied[skel_rows]
    return applied, coeffs


def leaf_down(leaf_args):
    applied, leaf_correction, ordering, skel_rows, inverse, leaf_base = leaf_args
    expanded = jnp.dot(leaf_base.astype(jnp.float32), rounded(leaf_correction))
    expanded = expanded.at[skel_rows].add(leaf_correction)
    solved = applied - jnp.dot(inverse.astype(jnp.float32), rounded(expanded))
    placed = jnp.zeros(solved.shape, jnp.bfloat16)
    return placed.at[ordering].set(solved.astype(jnp.bfloat16))


def reference(right_sides, point_order, skeleton, leaf_inverse, leaf_basis, group_core, transfer, top_core):
    side_leaves = right_sides.reshape(LEAVES, LEAF, RHS)
    inverse_leaves = leaf_inverse.reshape(LEAVES, LEAF, LEAF)
    basis_leaves = leaf_basis.reshape(LEAVES, LEAF, RANK)
    applied, coeffs = lax.map(leaf_up, (side_leaves, point_order, skeleton, inverse_leaves, basis_leaves))
    cores = group_core.reshape(N_AA, GROUP, GROUP).astype(jnp.float32)
    stacked = rounded(coeffs.reshape(N_AA, GROUP, RHS))
    level_one = jnp.einsum("agh,ahc->agc", cores, stacked, precision=lax.Precision.HIGHEST)
    level_one = level_one.reshape(LEAVES, RANK, RHS)
    remainder = coeffs - level_one
    transfer_leaves = transfer.reshape(LEAVES, RANK, RANK)
    partial_value = jnp.einsum("lrs,lrc->lsc", transfer_leaves, remainder, precision=lax.Precision.HIGHEST)
    group_coeffs = partial_value.reshape(N_AA, N_BA, RANK, RHS).sum(axis=1)
    top = jnp.dot(top_core.astype(jnp.float32), rounded(group_coeffs.reshape(TOP, RHS)), precision=lax.Precision.HIGHEST)
    top_leaves = jnp.broadcast_to(top.reshape(N_AA, 1, RANK, RHS), (N_AA, N_BA, RANK, RHS)).reshape(LEAVES, RANK, RHS)
    correction = level_one + jnp.einsum("lrs,lsc->lrc", transfer_leaves, top_leaves, precision=lax.Precision.HIGHEST)
    solved = lax.map(leaf_down, (applied, correction, point_order, skeleton, inverse_leaves, basis_leaves))
    return solved.reshape(POINTS, RHS)
```

```python
import functools

import jax
import jax.numpy as jnp
from jax import lax
from jax.experimental import pallas as pl
from jax.experimental.pallas import tpu as pltpu
from jax.sharding import PartitionSpec as P

MESH = pl.DeviceIdType.MESH
F32, BF16 = jnp.float32, jnp.bfloat16
LEAF, RANK, RHS = 1024, 128, 512
SIDE, NB, NZ = 4, 16, 16
PART = RHS // NB
REACH = 4


def dot(a, b):
    return jnp.dot(a, b, preferred_element_type=F32)


def wrap(value, n):
    return jnp.where(value >= n, value - n, value)


def kernel(
    sides_in, order_in, skel_in, inv_in, basis_in, core_in, trans_in, topc_in,
    out,
    sides, order, skel, inv, basis, core, trans, topc,
    point, point_t, pinv, ordered, applied, stretch,
    trans_all, coeff_all, part, part_all, topsel, top_rows, top_rows_t, core_t, zall, half, half_in, slices,
    in_sem, t_send, t_recv, x_sem, w_send, w_recv, r_send, r_recv, c_send, c_recv, z_send, z_recv, h_sem, s_send, s_recv,
):
    group, leaf = lax.axis_index("aa"), lax.axis_index("ba")
    at_z, half_id = group // 2, lax.rem(group, 2)
    at_x, at_y = leaf // SIDE, lax.rem(leaf, SIDE)
    partner = {"aa": group + 1 - 2 * half_id, "ba": leaf}
    peers = [{"aa": group, "ba": wrap(leaf + d, NB)} for d in range(1, NB)]

    def along_z(d):
        return {"aa": 2 * wrap(at_z + (d + NZ if d < 0 else d), NZ) + half_id, "ba": leaf}

    near = [d for k in range(REACH, 0, -1) for d in (k, -k)]

    loads = {}
    for i, (name, src, dst) in enumerate(
        (
            ("trans", trans_in, trans), ("order", order_in, order), ("skel", skel_in, skel), ("basis", basis_in, basis),
            ("inv", inv_in, inv), ("sides", sides_in, sides), ("topc", topc_in, topc), ("core", core_in, core),
        )
    ):
        loads[name] = pltpu.make_async_copy(src, dst, in_sem.at[i])
        loads[name].start()

    barrier = pltpu.get_barrier_semaphore()
    meet = [*peers, partner, *[along_z(d) for d in near]]
    for other in meet:
        pl.semaphore_signal(barrier, inc=1, device_id=other, device_id_type=MESH)

    def send(src, dst, send_sem, recv_sem, to):
        copy = pltpu.make_async_remote_copy(
            src_ref=src, dst_ref=dst, send_sem=send_sem, recv_sem=recv_sem, device_id=to, device_id_type=MESH
        )
        copy.start()
        return copy

    loads["trans"].wait()
    trans_all[leaf] = trans[...].astype(BF16)
    pl.semaphore_wait(barrier, len(meet))

    t_copies = [send(trans_all.at[leaf], trans_all.at[leaf], t_send.at[i], t_recv.at[i], to) for i, to in enumerate(peers)]

    loads["order"].wait()
    wanted = order[...].astype(F32)
    column = jnp.broadcast_to(wanted, (8, LEAF)).T[:, :1]
    point[...] = (column == lax.broadcasted_iota(jnp.int32, (LEAF, LEAF), 1).astype(F32)).astype(F32).astype(BF16)
    loads["skel"].wait()
    loads["basis"].wait()
    chosen = (lax.broadcasted_iota(jnp.int32, (LEAF, RANK), 0) == skel[...]).astype(F32)
    basis[...] = (basis[...].astype(F32) + chosen).astype(BF16)

    loads["topc"].wait()
    for k in range(NZ):
        topsel[:, k * RANK : (k + 1) * RANK] = topc[:, pl.ds(pl.multiple_of((2 * k + 1 - half_id) * RANK, RANK), RANK)]
        top_rows[half_id, leaf, :, k * RANK : (k + 1) * RANK] = topc[:, pl.ds(pl.multiple_of((2 * k + half_id) * RANK, RANK), RANK)]
    x_copy = send(topsel, top_rows.at[half_id, leaf], x_sem.at[0], x_sem.at[1], partner)

    loads["inv"].wait()
    reach = dot(basis[...].T, inv[...]).astype(BF16)
    gather = dot(reach, point[...]).astype(BF16)
    loads["sides"].wait()
    coeff_all[leaf] = dot(gather, sides[...]).T.astype(BF16)

    x_copy.wait_recv()
    w_copies = [
        send(top_rows.at[:, leaf], top_rows.at[:, leaf], w_send.at[i], w_recv.at[i], to) for i, to in enumerate(peers)
    ]

    loads["core"].wait()
    for copy in t_copies:
        copy.wait_recv()
    mixed = trans[...] - dot(core[...], trans_all[...].reshape(NB * RANK, RANK))
    part[...] = dot(coeff_all[leaf], mixed.astype(BF16)).astype(BF16).reshape(NB, PART, RANK)
    r_copies = []
    for i, to in enumerate(peers):
        r_copies.append(send(part.at[to["ba"]], part_all.at[leaf], r_send.at[i], r_recv.at[i], to))
    part_all[leaf] = part[leaf]

    full, quarter = RHS // 2, RHS // 4
    c_copies = {}

    def moved(along, step, place):
        x, y = place
        return (lax.rem(x + step + SIDE, SIDE), y) if along == 0 else (x, lax.rem(y + step + SIDE, SIDE))

    here = (at_x, at_y)

    def pass_on(key, place, low, count, along, step):
        block = place[0] * SIDE + place[1]
        to = moved(along, step, here)
        ref = coeff_all.at[block, pl.ds(low, count)]
        number = key[0] * 20 + key[1]
        c_copies[key] = send(ref, ref, c_send.at[number], c_recv.at[number], {"aa": group, "ba": to[0] * SIDE + to[1]})

    for h in (0, 1):
        first, second = (0, 1) if h == 0 else (1, 0)
        pass_on((h, 0), here, h * full, full, first, 1)
        pass_on((h, 1), here, h * full, full, first, -1)
        pass_on((h, 4), here, h * full, full, second, 1)
        pass_on((h, 5), here, h * full, full, second, -1)

    def c_first():
        for h in (0, 1):
            first, second = (0, 1) if h == 0 else (1, 0)
            for j, step in enumerate((-1, 1)):
                c_copies[h, j].wait_recv()
                place = moved(first, step, here)
                pass_on((h, 2 + j), place, h * full + j * quarter, quarter, first, -step)
                pass_on((h, 8 + 4 * j), place, h * full, full, second, 1)
                pass_on((h, 9 + 4 * j), place, h * full, full, second, -1)

    def c_across():
        for h in (0, 1):
            first, second = (0, 1) if h == 0 else (1, 0)
            c_copies[h, 2].wait_recv()
            c_copies[h, 3].wait_recv()
            place = moved(first, 2, here)
            pass_on((h, 16), place, h * full, full, second, 1)
            pass_on((h, 17), place, h * full, full, second, -1)

    def c_second(k, offset):
        for h in (0, 1):
            first, second = (0, 1) if h == 0 else (1, 0)
            for j, step in enumerate((-1, 1)):
                c_copies[h, 4 + 4 * k + j].wait_recv()
                place = moved(second, step, moved(first, offset, here))
                pass_on((h, 6 + 4 * k + j), place, h * full + j * quarter, quarter, second, -step)

    point_t[...] = (lax.broadcasted_iota(jnp.int32, (LEAF, LEAF), 0) == order[...]).astype(F32).astype(BF16)
    for i in range(2):
        rows = pl.ds(i * 512, 512)
        pinv[rows] = dot(point_t[rows], inv[...]).astype(BF16)

    for copy in r_copies:
        copy.wait_recv()
    total = jnp.sum(part_all[...].astype(F32), axis=0)
    zall[at_z] = total.astype(BF16)
    z_copies = {}
    for i, d in enumerate(near):
        z_copies[d] = send(zall.at[at_z], zall.at[at_z], z_send.at[i], z_recv.at[i], along_z(d))

    c_first()
    ordered[...] = dot(point[...], sides[...]).astype(BF16)
    c_across()

    relays = []
    for k in range(1, REACH + 1):
        for sign in (1, -1):
            z_copies[-sign * k].wait_recv()
            if sign < 0 and k == REACH:
                continue
            block = wrap(at_z + (sign * k if sign > 0 else NZ - k), NZ)
            n = 8 + len(relays)
            relays.append(send(zall.at[block], zall.at[block], z_send.at[n], z_recv.at[n], along_z(-sign * REACH)))

    c_second(0, 0)
    stretch_f = dot(pinv[...], basis[...])
    stretch[...] = stretch_f.astype(BF16)
    for copy in w_copies:
        copy.wait_recv()
    for k in range(2):
        top_rows_t[:, k * RANK : (k + 1) * RANK] = top_rows[k].reshape(RANK, NZ * RANK).T
    core_t[...] = core[...].T
    for copy in relays:
        copy.wait_recv()
    got = dot(jnp.concatenate([zall[k] for k in range(NZ)], axis=1), top_rows_t[...])
    half[0] = got[:, :RANK]
    half[1] = got[:, RANK:]
    h_copy = send(half.at[1 - half_id], half_in, h_sem.at[0], h_sem.at[1], partner)
    h_copy.wait_recv()
    slices[leaf] = (half[half_id] + half_in[...]).astype(BF16)
    s_copies = [send(slices.at[leaf], slices.at[leaf], s_send.at[i], s_recv.at[i], to) for i, to in enumerate(peers)]

    c_second(1, -1)
    c_second(2, 1)
    c_second(3, 2)
    for h in (0, 1):
        for k in range(4):
            c_copies[h, 6 + 4 * k].wait_recv()
            c_copies[h, 7 + 4 * k].wait_recv()
    level = dot(jnp.concatenate([coeff_all[k] for k in range(NB)], axis=1), core_t[...])
    spread = dot(stretch[...], trans[...].astype(BF16)).astype(BF16)
    lowered = level.astype(BF16).T
    for i in range(2):
        rows = pl.ds(i * 512, 512)
        applied[rows] = dot(pinv[rows], ordered[...]) - dot(stretch[rows], lowered)

    for copy in s_copies:
        copy.wait_recv()
    top = slices[...].reshape(RHS, RANK).T
    out[...] = (applied[...] - dot(spread, top)).astype(BF16)

    for copy in (*t_copies, x_copy, *w_copies, *r_copies, *c_copies.values(), *z_copies.values(), *relays, h_copy, *s_copies):
        copy.wait_send()


def shards(*args):
    dma = pltpu.SemaphoreType.DMA
    vmem = pltpu.VMEM
    scratch = [
        vmem((LEAF, RHS), BF16), vmem((1, LEAF), jnp.int32), vmem((1, RANK), jnp.int32), vmem((LEAF, LEAF), BF16),
        vmem((LEAF, RANK), BF16), vmem((RANK, NB * RANK), BF16), vmem((RANK, RANK), F32), vmem((8, 2 * NZ * RANK), BF16),
        vmem((LEAF, LEAF), BF16), vmem((LEAF, LEAF), BF16), vmem((LEAF, LEAF), BF16), vmem((LEAF, RHS), BF16),
        vmem((LEAF, RHS), F32), vmem((LEAF, RANK), BF16),
        vmem((NB, RANK, RANK), BF16), vmem((NB, RHS, RANK), BF16), vmem((NB, PART, RANK), BF16), vmem((NB, PART, RANK), BF16),
        vmem((8, NZ * RANK), BF16), vmem((2, NB, 8, NZ * RANK), BF16), vmem((NZ * RANK, 2 * RANK), BF16),
        vmem((NB * RANK, RANK), BF16), vmem((NZ, PART, RANK), BF16), vmem((2, PART, RANK), F32), vmem((PART, RANK), F32),
        vmem((NB, PART, RANK), BF16),
        dma((8,)), dma((15,)), dma((15,)), dma((2,)), dma((15,)), dma((15,)), dma((15,)), dma((15,)),
        dma((40,)), dma((40,)), dma((15,)), dma((15,)), dma((2,)), dma((15,)), dma((15,)),
    ]
    return pl.pallas_call(
        kernel,
        out_shape=jax.ShapeDtypeStruct((LEAF, RHS), BF16),
        in_specs=[pl.BlockSpec(memory_space=pl.ANY)] * 8,
        out_specs=pl.BlockSpec(memory_space=pltpu.VMEM),
        scratch_shapes=scratch,
        compiler_params=pltpu.CompilerParams(collective_id=0, has_side_effects=True, vmem_limit_bytes=67043328),
        name="woodbury",
    )(*args)


def solution(mesh):
    split = P(("aa", "ba"), None)
    return jax.shard_map(shards, mesh=mesh, in_specs=(split,) * 8, out_specs=split, check_vma=False)
```

```python
import functools

import jax
import jax.numpy as jnp
from jax import lax
from jax.experimental import pallas as pl
from jax.experimental.pallas import tpu as pltpu
from jax.sharding import PartitionSpec as P

MESH = pl.DeviceIdType.MESH
F32, BF16 = jnp.float32, jnp.bfloat16
LEAF, RANK, RHS = 1024, 128, 512
SIDE, NB, NZ = 4, 16, 16
PART = RHS // NB


def dot(a, b):
    return jnp.dot(a, b, preferred_element_type=F32)


def wrap(value, n):
    return jnp.where(value >= n, value - n, value)


def kernel(
    sides_in, order_in, skel_in, inv_in, basis_in, core_in, trans_in, topc_in,
    out,
    sides, order, skel, inv, basis, core, trans, topc,
    point, point_t, pinv, ordered, applied, stretch,
    trans_all, coeff_all, part, part_all, topsel, top_rows, top_rows_t, core_t, zall, half, half_in, slices,
    in_sem, send_sem, t_recv, x_sem, w_recv, r_recv, c_recv, z_recv, s_recv, known_sem,
):
    group, leaf = lax.axis_index("aa"), lax.axis_index("ba")
    at_z, half_id = group // 2, lax.rem(group, 2)
    at_x, at_y = leaf // SIDE, lax.rem(leaf, SIDE)
    partner = {"aa": group + 1 - 2 * half_id, "ba": leaf}
    peers = [{"aa": group, "ba": wrap(leaf + d, NB)} for d in range(1, NB)]

    def along_z(d):
        return {"aa": 2 * wrap(at_z + (d + NZ if d < 0 else d), NZ) + half_id, "ba": leaf}

    loads = {}
    for i, (name, src, dst) in enumerate(
        (
            ("trans", trans_in, trans), ("order", order_in, order), ("skel", skel_in, skel), ("topc", topc_in, topc),
            ("basis", basis_in, basis), ("inv", inv_in, inv), ("sides", sides_in, sides), ("core", core_in, core),
        )
    ):
        loads[name] = pltpu.make_async_copy(src, dst, in_sem.at[i])
        loads[name].start()

    def signal(sem, to):
        pl.semaphore_signal(sem, inc=1, device_id=to, device_id_type=MESH)

    barrier = pltpu.get_barrier_semaphore()
    meet = [*peers, partner, along_z(1), along_z(-1)]
    for other in meet:
        signal(barrier, other)

    def send(src, dst, send_sem, recv_sem, to):
        pltpu.make_async_remote_copy(
            src_ref=src, dst_ref=dst, send_sem=send_sem, recv_sem=recv_sem, device_id=to, device_id_type=MESH
        ).start()

    def taken(ref, sem):
        pltpu.make_async_copy(ref, ref, sem).wait()

    here = (at_x, at_y)

    def moved(along, step, place):
        x, y = place
        return (lax.rem(x + step + SIDE, SIDE), y) if along == 0 else (x, lax.rem(y + step + SIDE, SIDE))

    def index(place):
        return place[0] * SIDE + place[1]

    loads["trans"].wait()
    trans_all[leaf] = trans[...].astype(BF16)
    pl.semaphore_wait(barrier, len(meet))

    for to in peers:
        send(trans_all.at[leaf], trans_all.at[leaf], send_sem.at[0], t_recv.at[0], to)
    signal(known_sem.at[0], along_z(1))
    signal(known_sem.at[0], along_z(-1))

    loads["topc"].wait()
    for k in range(NZ):
        topsel[:, k * RANK : (k + 1) * RANK] = topc[:, pl.ds(pl.multiple_of((2 * k + 1 - half_id) * RANK, RANK), RANK)]
        top_rows[half_id, leaf, :, k * RANK : (k + 1) * RANK] = topc[:, pl.ds(pl.multiple_of((2 * k + half_id) * RANK, RANK), RANK)]
    send(topsel, top_rows.at[half_id, leaf], send_sem.at[1], x_sem.at[0], partner)

    loads["order"].wait()
    wanted = order[...].astype(F32)
    column = jnp.broadcast_to(wanted, (8, LEAF)).T[:, :1]
    point[...] = (column == lax.broadcasted_iota(jnp.int32, (LEAF, LEAF), 1).astype(F32)).astype(F32).astype(BF16)
    loads["skel"].wait()
    loads["basis"].wait()
    chosen = (lax.broadcasted_iota(jnp.int32, (LEAF, RANK), 0) == skel[...]).astype(F32)
    basis[...] = (basis[...].astype(F32) + chosen).astype(BF16)

    class Gather:
        def __init__(self, piece, some, send_sem, recv_sem):
            self.piece, self.some, self.out_sem, self.in_sem = piece, some, send_sem, recv_sem

        def put(self, h, sem, place, part, along, step):
            ref = self.piece(h, index(place), part)
            send(ref, ref, self.out_sem, self.in_sem.at[sem], {"aa": group, "ba": index(moved(along, step, here))})

        def near(self):
            for h in (0, 1):
                for step in (1, -1):
                    self.put(h, 0, here, None, h, step)

        def relay_near(self):
            taken(self.some(2), self.in_sem.at[0])
            for h in (0, 1):
                for j, step in enumerate((-1, 1)):
                    self.put(h, 1, moved(h, step, here), j, h, -step)

        def over(self, k):
            if k == 3:
                taken(self.some(1), self.in_sem.at[1])
            for h in (0, 1):
                for step in (1, -1):
                    self.put(h, 2 + k, moved(h, (0, -1, 1, 2)[k], here), None, 1 - h, step)

        def relay_over(self, k):
            taken(self.some(2), self.in_sem.at[2 + k])
            for h in (0, 1):
                for j, step in enumerate((-1, 1)):
                    self.put(h, 6, moved(1 - h, step, moved(h, (0, -1, 1, 2)[k], here)), j, 1 - h, -step)

        def finish(self):
            taken(self.some(4), self.in_sem.at[6])

    full, quarter, columns = RHS // 2, RHS // 4, NZ * RANK // 2

    def coeff_piece(h, block, part):
        return coeff_all.at[block, pl.ds(h * full, full) if part is None else pl.ds(h * full + part * quarter, quarter)]

    def top_piece(h, block, part):
        return top_rows.at[h, block] if part is None else top_rows.at[h, block, :, pl.ds(part * columns, columns)]

    of_coeffs = Gather(coeff_piece, lambda n: coeff_all.at[pl.ds(0, n)], send_sem.at[2], c_recv)
    of_top = Gather(top_piece, lambda n: top_rows.at[:, pl.ds(0, n)], send_sem.at[3], w_recv)

    loads["inv"].wait()
    reach = dot(basis[...].T, inv[...]).astype(BF16)
    gather = dot(reach, point[...]).astype(BF16)
    loads["sides"].wait()
    coeff_all[leaf] = dot(gather, sides[...]).T.astype(BF16)

    taken(top_rows.at[0, 0], x_sem.at[0])
    of_top.near()
    of_top.over(0)
    of_coeffs.near()
    pl.semaphore_wait(known_sem.at[0], 2)
    signal(known_sem.at[1], along_z(2))
    signal(known_sem.at[1], along_z(-2))

    loads["core"].wait()
    taken(trans_all.at[pl.ds(0, NB - 1)], t_recv.at[0])
    mixed = trans[...] - dot(core[...], trans_all[...].reshape(NB * RANK, RANK))
    part[...] = dot(coeff_all[leaf], mixed.astype(BF16)).astype(BF16).reshape(NB, PART, RANK)
    for to in peers:
        send(part.at[to["ba"]], part_all.at[leaf], send_sem.at[4], r_recv.at[0], to)
    part_all[leaf] = part[leaf]
    pl.semaphore_wait(known_sem.at[1], 2)
    signal(known_sem.at[2], along_z(4))
    signal(known_sem.at[2], along_z(-4))
    of_top.relay_near()
    of_top.over(1)
    of_top.over(2)

    point_t[...] = (lax.broadcasted_iota(jnp.int32, (LEAF, LEAF), 0) == order[...]).astype(F32).astype(BF16)
    for i in range(2):
        rows = pl.ds(i * 512, 512)
        pinv[rows] = dot(point_t[rows], inv[...]).astype(BF16)
    of_top.over(3)
    for k in range(3):
        of_top.relay_over(k)
    of_coeffs.relay_near()
    core_t[...] = core[...].T
    pl.semaphore_wait(known_sem.at[2], 2)

    taken(part_all.at[pl.ds(0, NB - 1)], r_recv.at[0])
    total = jnp.sum(part_all[...].astype(F32), axis=0)
    zall[at_z] = total.astype(BF16)
    for d in (NZ // 2, *[d for k in range(NZ // 2 - 1, 0, -1) for d in (k, -k)]):
        send(zall.at[at_z], zall.at[at_z], send_sem.at[5], z_recv.at[0], along_z(d))

    for k in range(3):
        of_coeffs.over(k)
    ordered[...] = dot(point[...], sides[...]).astype(BF16)
    of_top.relay_over(3)
    stretch[...] = dot(pinv[...], basis[...]).astype(BF16)
    of_coeffs.over(3)

    for i in range(2):
        rows = pl.ds(i * 512, 512)
        applied[rows] = dot(pinv[rows], ordered[...])
    spread = dot(stretch[...], trans[...].astype(BF16)).astype(BF16)
    of_top.finish()
    for k in range(2):
        top_rows_t[:, k * RANK : (k + 1) * RANK] = top_rows[k].reshape(RANK, NZ * RANK).T
    for k in range(3):
        of_coeffs.relay_over(k)
    taken(zall.at[pl.ds(0, NZ - 1)], z_recv.at[0])
    got = dot(jnp.concatenate([zall[k] for k in range(NZ)], axis=1), top_rows_t[...])
    half[0] = got[:, :RANK]
    half[1] = got[:, RANK:]
    send(half.at[1 - half_id], half_in, send_sem.at[6], x_sem.at[1], partner)
    of_coeffs.relay_over(3)
    taken(half_in, x_sem.at[1])
    slices[leaf] = (half[half_id] + half_in[...]).astype(BF16)
    for to in peers:
        send(slices.at[leaf], slices.at[leaf], send_sem.at[7], s_recv.at[0], to)

    of_coeffs.finish()
    lowered = dot(jnp.concatenate([coeff_all[k] for k in range(NB)], axis=1), core_t[...]).astype(BF16).T
    applied[...] -= dot(stretch[...], lowered)
    for i, ref in enumerate(
        (
            trans_all.at[pl.ds(0, NB - 1)], topsel, coeff_all.at[pl.ds(0, NB - 1)], top_rows.at[:, pl.ds(0, NB - 1)],
            part_all.at[pl.ds(0, NB - 1)], zall.at[pl.ds(0, NZ - 1)], half_in,
        )
    ):
        taken(ref, send_sem.at[i])

    taken(slices.at[pl.ds(0, NB - 1)], s_recv.at[0])
    top = slices[...].reshape(RHS, RANK).T
    out[...] = (applied[...] - dot(spread, top)).astype(BF16)
    taken(slices.at[pl.ds(0, NB - 1)], send_sem.at[7])


def shards(*args):
    dma = pltpu.SemaphoreType.DMA
    vmem = pltpu.VMEM
    scratch = [
        vmem((LEAF, RHS), BF16), vmem((1, LEAF), jnp.int32), vmem((1, RANK), jnp.int32), vmem((LEAF, LEAF), BF16),
        vmem((LEAF, RANK), BF16), vmem((RANK, NB * RANK), BF16), vmem((RANK, RANK), F32), vmem((8, 2 * NZ * RANK), BF16),
        vmem((LEAF, LEAF), BF16), vmem((LEAF, LEAF), BF16), vmem((LEAF, LEAF), BF16), vmem((LEAF, RHS), BF16),
        vmem((LEAF, RHS), F32), vmem((LEAF, RANK), BF16),
        vmem((NB, RANK, RANK), BF16), vmem((NB, RHS, RANK), BF16), vmem((NB, PART, RANK), BF16), vmem((NB, PART, RANK), BF16),
        vmem((8, NZ * RANK), BF16), vmem((2, NB, 8, NZ * RANK), BF16), vmem((NZ * RANK, 2 * RANK), BF16),
        vmem((NB * RANK, RANK), BF16), vmem((NZ, PART, RANK), BF16), vmem((2, PART, RANK), F32), vmem((PART, RANK), F32),
        vmem((NB, PART, RANK), BF16),
        dma((8,)), dma((8,)), dma((1,)), dma((2,)), dma((7,)), dma((1,)), dma((7,)), dma((1,)), dma((1,)),
        pltpu.SemaphoreType.REGULAR((3,)),
    ]
    return pl.pallas_call(
        kernel,
        out_shape=jax.ShapeDtypeStruct((LEAF, RHS), BF16),
        in_specs=[pl.BlockSpec(memory_space=pl.ANY)] * 8,
        out_specs=pl.BlockSpec(memory_space=pltpu.VMEM),
        scratch_shapes=scratch,
        compiler_params=pltpu.CompilerParams(collective_id=0, has_side_effects=True, vmem_limit_bytes=40 * 2**20),
        name="woodbury",
    )(*[pltpu.with_memory_space_constraint(a, pltpu.HBM) for a in args])


def solution(mesh):
    split = P(("aa", "ba"), None)
    return jax.shard_map(shards, mesh=mesh, in_specs=(split,) * 8, out_specs=split, check_vma=False)
```

```python
import functools

import jax
import jax.numpy as jnp
from jax import lax
from jax.experimental import pallas as pl
from jax.experimental.pallas import tpu as pltpu
from jax.sharding import PartitionSpec as P

MESH = pl.DeviceIdType.MESH
F32, BF16 = jnp.float32, jnp.bfloat16
LEAF, RANK, RHS = 1024, 128, 512
SIDE, NB, NZ = 4, 16, 16
PART = RHS // NB


def dot(a, b):
    return jnp.dot(a, b, preferred_element_type=F32)


def wrap(value, n):
    return jnp.where(value >= n, value - n, value)


def kernel(
    sides_in, order_in, skel_in, inv_in, basis_in, core_in, trans_in, topc_in,
    out,
    sides, order, skel, inv, basis, core, trans, topc,
    point, point_t, pinv, ordered, applied, stretch,
    trans_all, coeff_all, part, part_all, topsel, top_rows, top_rows_t, core_t, zall, half, half_in, slices,
    in_sem, send_sem, t_recv, x_sem, w_recv, r_recv, c_recv, z_recv, s_recv, known_sem,
):
    group, leaf = lax.axis_index("aa"), lax.axis_index("ba")
    at_z, half_id = group // 2, lax.rem(group, 2)
    at_x, at_y = leaf // SIDE, lax.rem(leaf, SIDE)
    partner = {"aa": group + 1 - 2 * half_id, "ba": leaf}
    def index(place):
        return place[0] * SIDE + place[1]

    far = [(2, 2), (2, 1), (2, 3), (1, 2), (3, 2), (2, 0), (0, 2), (1, 1), (3, 3), (1, 3), (3, 1), (1, 0), (3, 0), (0, 1), (0, 3)]
    peers = [{"aa": group, "ba": index((wrap(at_x + dx, SIDE), wrap(at_y + dy, SIDE)))} for dx, dy in far]

    def along_z(d):
        return {"aa": 2 * wrap(at_z + (d + NZ if d < 0 else d), NZ) + half_id, "ba": leaf}

    loads = {}
    for i, (name, src, dst) in enumerate(
        (
            ("trans", trans_in, trans), ("order", order_in, order), ("skel", skel_in, skel), ("topc", topc_in, topc),
            ("basis", basis_in, basis), ("inv", inv_in, inv), ("sides", sides_in, sides), ("core", core_in, core),
        )
    ):
        loads[name] = pltpu.make_async_copy(src, dst, in_sem.at[i])
        loads[name].start()

    def signal(sem, to):
        pl.semaphore_signal(sem, inc=1, device_id=to, device_id_type=MESH)

    barrier = pltpu.get_barrier_semaphore()
    meet = [*peers, partner, along_z(1), along_z(-1)]
    for other in meet:
        signal(barrier, other)

    def send(src, dst, send_sem, recv_sem, to):
        pltpu.make_async_remote_copy(
            src_ref=src, dst_ref=dst, send_sem=send_sem, recv_sem=recv_sem, device_id=to, device_id_type=MESH
        ).start()

    def taken(ref, sem):
        pltpu.make_async_copy(ref, ref, sem).wait()

    here = (at_x, at_y)

    def moved(along, step, place):
        x, y = place
        return (lax.rem(x + step + SIDE, SIDE), y) if along == 0 else (x, lax.rem(y + step + SIDE, SIDE))

    loads["trans"].wait()
    trans_all[leaf] = trans[...].astype(BF16)
    pl.semaphore_wait(barrier, len(meet))

    for to in peers:
        send(trans_all.at[leaf], trans_all.at[leaf], send_sem.at[0], t_recv.at[0], to)
    signal(known_sem.at[0], along_z(1))
    signal(known_sem.at[0], along_z(-1))

    loads["topc"].wait()
    for k in range(NZ):
        topsel[:, k * RANK : (k + 1) * RANK] = topc[:, pl.ds(pl.multiple_of((2 * k + 1 - half_id) * RANK, RANK), RANK)]
        top_rows[half_id, leaf, :, k * RANK : (k + 1) * RANK] = topc[:, pl.ds(pl.multiple_of((2 * k + half_id) * RANK, RANK), RANK)]
    send(topsel, top_rows.at[half_id, leaf], send_sem.at[1], x_sem.at[0], partner)

    loads["order"].wait()
    wanted = order[...].astype(F32)
    column = jnp.broadcast_to(wanted, (8, LEAF)).T[:, :1]
    point[...] = (column == lax.broadcasted_iota(jnp.int32, (LEAF, LEAF), 1).astype(F32)).astype(F32).astype(BF16)
    loads["skel"].wait()
    loads["basis"].wait()
    chosen = (lax.broadcasted_iota(jnp.int32, (LEAF, RANK), 0) == skel[...]).astype(F32)
    basis[...] = (basis[...].astype(F32) + chosen).astype(BF16)

    class Gather:
        def __init__(self, piece, some, send_sem, recv_sem):
            self.piece, self.some, self.out_sem, self.in_sem = piece, some, send_sem, recv_sem

        def put(self, h, sem, place, part, along, step):
            ref = self.piece(h, index(place), part)
            send(ref, ref, self.out_sem, self.in_sem.at[sem], {"aa": group, "ba": index(moved(along, step, here))})

        def near(self):
            for h in (0, 1):
                for step in (1, -1):
                    self.put(h, 0, here, None, h, step)

        def relay_near(self):
            taken(self.some(2), self.in_sem.at[0])
            for h in (0, 1):
                for j, step in enumerate((-1, 1)):
                    self.put(h, 1, moved(h, step, here), j, h, -step)

        def over(self, k):
            if k == 3:
                taken(self.some(1), self.in_sem.at[1])
            for h in (0, 1):
                for step in (1, -1):
                    self.put(h, 2 + k, moved(h, (0, -1, 1, 2)[k], here), None, 1 - h, step)

        def relay_over(self, k):
            taken(self.some(2), self.in_sem.at[2 + k])
            for h in (0, 1):
                for j, step in enumerate((-1, 1)):
                    self.put(h, 6, moved(1 - h, step, moved(h, (0, -1, 1, 2)[k], here)), j, 1 - h, -step)

        def finish(self):
            taken(self.some(4), self.in_sem.at[6])

    full, quarter, columns = RHS // 2, RHS // 4, NZ * RANK // 2

    def coeff_piece(h, block, part):
        return coeff_all.at[block, pl.ds(h * full, full) if part is None else pl.ds(h * full + part * quarter, quarter)]

    def top_piece(h, block, part):
        return top_rows.at[h, block] if part is None else top_rows.at[h, block, :, pl.ds(part * columns, columns)]

    of_coeffs = Gather(coeff_piece, lambda n: coeff_all.at[pl.ds(0, n)], send_sem.at[2], c_recv)
    of_top = Gather(top_piece, lambda n: top_rows.at[:, pl.ds(0, n)], send_sem.at[3], w_recv)

    loads["inv"].wait()
    reach = dot(basis[...].T, inv[...]).astype(BF16)
    gather = dot(reach, point[...]).astype(BF16)
    loads["sides"].wait()
    coeff_all[leaf] = dot(gather, sides[...]).T.astype(BF16)

    taken(top_rows.at[0, 0], x_sem.at[0])
    of_top.near()
    of_coeffs.near()
    pl.semaphore_wait(known_sem.at[0], 2)
    signal(known_sem.at[1], along_z(2))
    signal(known_sem.at[1], along_z(-2))

    loads["core"].wait()
    taken(trans_all.at[pl.ds(0, NB - 1)], t_recv.at[0])
    mixed = trans[...] - dot(core[...], trans_all[...].reshape(NB * RANK, RANK))
    part[...] = dot(coeff_all[leaf], mixed.astype(BF16)).astype(BF16).reshape(NB, PART, RANK)
    for to in peers:
        send(part.at[to["ba"]], part_all.at[leaf], send_sem.at[4], r_recv.at[0], to)
    part_all[leaf] = part[leaf]
    pl.semaphore_wait(known_sem.at[1], 2)
    signal(known_sem.at[2], along_z(4))
    signal(known_sem.at[2], along_z(-4))
    of_top.over(0)
    of_top.relay_near()
    of_top.over(1)
    of_top.over(2)

    point_t[...] = (lax.broadcasted_iota(jnp.int32, (LEAF, LEAF), 0) == order[...]).astype(F32).astype(BF16)
    for i in range(2):
        rows = pl.ds(i * 512, 512)
        pinv[rows] = dot(point_t[rows], inv[...]).astype(BF16)
    of_coeffs.relay_near()
    core_t[...] = core[...].T
    pl.semaphore_wait(known_sem.at[2], 2)

    taken(part_all.at[pl.ds(0, NB - 1)], r_recv.at[0])
    total = jnp.sum(part_all[...].astype(F32), axis=0)
    zall[at_z] = total.astype(BF16)
    for d in (NZ // 2, *[d for k in range(NZ // 2 - 1, 0, -1) for d in (k, -k)]):
        send(zall.at[at_z], zall.at[at_z], send_sem.at[5], z_recv.at[0], along_z(d))

    of_top.over(3)
    for k in range(3):
        of_top.relay_over(k)
    for k in range(3):
        of_coeffs.over(k)
    ordered[...] = dot(point[...], sides[...]).astype(BF16)
    of_top.relay_over(3)
    stretch[...] = dot(pinv[...], basis[...]).astype(BF16)
    of_coeffs.over(3)

    for i in range(2):
        rows = pl.ds(i * 512, 512)
        applied[rows] = dot(pinv[rows], ordered[...])
    spread = dot(stretch[...], trans[...].astype(BF16)).astype(BF16)
    of_top.finish()
    for k in range(2):
        top_rows_t[:, k * RANK : (k + 1) * RANK] = top_rows[k].reshape(RANK, NZ * RANK).T
    for k in range(3):
        of_coeffs.relay_over(k)
    taken(zall.at[pl.ds(0, NZ - 1)], z_recv.at[0])
    got = dot(jnp.concatenate([zall[k] for k in range(NZ)], axis=1), top_rows_t[...])
    half[0] = got[:, :RANK]
    half[1] = got[:, RANK:]
    send(half.at[1 - half_id], half_in, send_sem.at[6], x_sem.at[1], partner)
    of_coeffs.relay_over(3)
    taken(half_in, x_sem.at[1])
    slices[leaf] = (half[half_id] + half_in[...]).astype(BF16)
    for to in peers:
        send(slices.at[leaf], slices.at[leaf], send_sem.at[7], s_recv.at[0], to)

    def of_blocks(h, steps):
        blocks = [index(moved(1 - h, step, moved(h, other, here))) for step in steps for other in range(SIDE)]
        left = jnp.concatenate([coeff_all[k, h * full : (h + 1) * full] for k in blocks], axis=1)
        return dot(left, jnp.concatenate([core_t[pl.ds(pl.multiple_of(k * RANK, RANK), RANK)] for k in blocks], axis=0))

    early = [of_blocks(h, (0, 1, -1)) for h in (0, 1)]
    of_coeffs.finish()
    lowered = jnp.concatenate([early[h] + of_blocks(h, (2,)) for h in (0, 1)], axis=0).astype(BF16).T
    applied[...] -= dot(stretch[...], lowered)
    for i, ref in enumerate(
        (
            trans_all.at[pl.ds(0, NB - 1)], topsel, coeff_all.at[pl.ds(0, NB - 1)], top_rows.at[:, pl.ds(0, NB - 1)],
            part_all.at[pl.ds(0, NB - 1)], zall.at[pl.ds(0, NZ - 1)], half_in,
        )
    ):
        taken(ref, send_sem.at[i])

    taken(slices.at[pl.ds(0, NB - 1)], s_recv.at[0])
    top = slices[...].reshape(RHS, RANK).T
    out[...] = (applied[...] - dot(spread, top)).astype(BF16)
    taken(slices.at[pl.ds(0, NB - 1)], send_sem.at[7])


def shards(*args):
    dma = pltpu.SemaphoreType.DMA
    vmem = pltpu.VMEM
    scratch = [
        vmem((LEAF, RHS), BF16), vmem((1, LEAF), jnp.int32), vmem((1, RANK), jnp.int32), vmem((LEAF, LEAF), BF16),
        vmem((LEAF, RANK), BF16), vmem((RANK, NB * RANK), BF16), vmem((RANK, RANK), F32), vmem((8, 2 * NZ * RANK), BF16),
        vmem((LEAF, LEAF), BF16), vmem((LEAF, LEAF), BF16), vmem((LEAF, LEAF), BF16), vmem((LEAF, RHS), BF16),
        vmem((LEAF, RHS), F32), vmem((LEAF, RANK), BF16),
        vmem((NB, RANK, RANK), BF16), vmem((NB, RHS, RANK), BF16), vmem((NB, PART, RANK), BF16), vmem((NB, PART, RANK), BF16),
        vmem((8, NZ * RANK), BF16), vmem((2, NB, 8, NZ * RANK), BF16), vmem((NZ * RANK, 2 * RANK), BF16),
        vmem((NB * RANK, RANK), BF16), vmem((NZ, PART, RANK), BF16), vmem((2, PART, RANK), F32), vmem((PART, RANK), F32),
        vmem((NB, PART, RANK), BF16),
        dma((8,)), dma((8,)), dma((1,)), dma((2,)), dma((7,)), dma((1,)), dma((7,)), dma((1,)), dma((1,)),
        pltpu.SemaphoreType.REGULAR((3,)),
    ]
    return pl.pallas_call(
        kernel,
        out_shape=jax.ShapeDtypeStruct((LEAF, RHS), BF16),
        in_specs=[pl.BlockSpec(memory_space=pl.ANY)] * 8,
        out_specs=pl.BlockSpec(memory_space=pltpu.VMEM),
        scratch_shapes=scratch,
        compiler_params=pltpu.CompilerParams(collective_id=0, has_side_effects=True, vmem_limit_bytes=40 * 2**20),
        name="woodbury",
    )(*[pltpu.with_memory_space_constraint(a, pltpu.HBM) for a in args])


def solution(mesh):
    split = P(("aa", "ba"), None)
    return jax.shard_map(shards, mesh=mesh, in_specs=(split,) * 8, out_specs=split, check_vma=False)
```

```python
import functools

import jax
import jax.numpy as jnp
from jax import lax
from jax.experimental import pallas as pl
from jax.experimental.pallas import tpu as pltpu
from jax.sharding import PartitionSpec as P

MESH = pl.DeviceIdType.MESH
F32, BF16 = jnp.float32, jnp.bfloat16
LEAF, RANK, RHS = 1024, 128, 512
SIDE, NB, NZ = 4, 16, 16
PART = RHS // NB


def dot(a, b):
    return jnp.dot(a, b, preferred_element_type=F32)


def wrap(value, n):
    return jnp.where(value >= n, value - n, value)


def kernel(
    sides_in, order_in, skel_in, inv_in, basis_in, core_in, trans_in, topc_in,
    out,
    sides, order, skel, inv, basis, core, trans, topc,
    point, point_t, pinv, ordered, applied, stretch,
    trans_all, coeff_all, part, part_all, topsel, top_rows, top_rows_t, core_t, zall, half, half_in, slices,
    in_sem, send_sem, t_recv, x_sem, w_recv, r_recv, c_recv, z_recv, s_recv, known_sem,
):
    group, leaf = lax.axis_index("aa"), lax.axis_index("ba")
    at_z, half_id = group // 2, lax.rem(group, 2)
    at_x, at_y = leaf // SIDE, lax.rem(leaf, SIDE)
    partner = {"aa": group + 1 - 2 * half_id, "ba": leaf}
    def index(place):
        return place[0] * SIDE + place[1]

    far = [(2, 2), (2, 1), (2, 3), (1, 2), (3, 2), (2, 0), (0, 2), (1, 1), (3, 3), (1, 3), (3, 1), (1, 0), (3, 0), (0, 1), (0, 3)]
    peers = [{"aa": group, "ba": index((wrap(at_x + dx, SIDE), wrap(at_y + dy, SIDE)))} for dx, dy in far]

    def along_z(d):
        return {"aa": 2 * wrap(at_z + (d + NZ if d < 0 else d), NZ) + half_id, "ba": leaf}

    loads = {}
    for i, (name, src, dst) in enumerate(
        (
            ("trans", trans_in, trans), ("order", order_in, order), ("skel", skel_in, skel), ("topc", topc_in, topc),
            ("basis", basis_in, basis), ("inv", inv_in, inv), ("sides", sides_in, sides), ("core", core_in, core),
        )
    ):
        loads[name] = pltpu.make_async_copy(src, dst, in_sem.at[i])
        loads[name].start()

    def signal(sem, to):
        pl.semaphore_signal(sem, inc=1, device_id=to, device_id_type=MESH)

    barrier = pltpu.get_barrier_semaphore()
    meet = [*peers, partner, along_z(1), along_z(-1)]
    for other in meet:
        signal(barrier, other)

    def send(src, dst, send_sem, recv_sem, to):
        pltpu.make_async_remote_copy(
            src_ref=src, dst_ref=dst, send_sem=send_sem, recv_sem=recv_sem, device_id=to, device_id_type=MESH
        ).start()

    def taken(ref, sem):
        pltpu.make_async_copy(ref, ref, sem).wait()

    here = (at_x, at_y)

    def moved(along, step, place):
        x, y = place
        return (lax.rem(x + step + SIDE, SIDE), y) if along == 0 else (x, lax.rem(y + step + SIDE, SIDE))

    loads["trans"].wait()
    trans_all[leaf] = trans[...].astype(BF16)
    pl.semaphore_wait(barrier, len(meet))

    for to in peers:
        send(trans_all.at[leaf], trans_all.at[leaf], send_sem.at[0], t_recv.at[0], to)
    signal(known_sem.at[0], along_z(1))
    signal(known_sem.at[0], along_z(-1))

    loads["topc"].wait()
    for k in range(NZ):
        topsel[:, k * RANK : (k + 1) * RANK] = topc[:, pl.ds(pl.multiple_of((2 * k + 1 - half_id) * RANK, RANK), RANK)]
        top_rows[half_id, leaf, :, k * RANK : (k + 1) * RANK] = topc[:, pl.ds(pl.multiple_of((2 * k + half_id) * RANK, RANK), RANK)]
    send(topsel, top_rows.at[half_id, leaf], send_sem.at[1], x_sem.at[0], partner)

    loads["order"].wait()
    wanted = order[...].astype(F32)
    column = jnp.broadcast_to(wanted, (8, LEAF)).T[:, :1]
    point[...] = (column == lax.broadcasted_iota(jnp.int32, (LEAF, LEAF), 1).astype(F32)).astype(F32).astype(BF16)
    loads["skel"].wait()
    loads["basis"].wait()
    chosen = (lax.broadcasted_iota(jnp.int32, (LEAF, RANK), 0) == skel[...]).astype(F32)
    basis[...] = (basis[...].astype(F32) + chosen).astype(BF16)

    class Gather:
        def __init__(self, piece, some, send_sem, recv_sem):
            self.piece, self.some, self.out_sem, self.in_sem = piece, some, send_sem, recv_sem

        def put(self, h, sem, place, part, along, step):
            ref = self.piece(h, index(place), part)
            send(ref, ref, self.out_sem, self.in_sem.at[sem], {"aa": group, "ba": index(moved(along, step, here))})

        def near(self):
            for h in (0, 1):
                for step in (1, -1):
                    self.put(h, 0, here, None, h, step)

        def relay_near(self):
            taken(self.some(2), self.in_sem.at[0])
            for h in (0, 1):
                for j, step in enumerate((-1, 1)):
                    self.put(h, 1, moved(h, step, here), j, h, -step)

        def over(self, k):
            if k == 3:
                taken(self.some(1), self.in_sem.at[1])
            for h in (0, 1):
                for step in (1, -1):
                    self.put(h, 2 + k, moved(h, (0, -1, 1, 2)[k], here), None, 1 - h, step)

        def relay_over(self, k):
            taken(self.some(2), self.in_sem.at[2 + k])
            for h in (0, 1):
                for j, step in enumerate((-1, 1)):
                    self.put(h, 6, moved(1 - h, step, moved(h, (0, -1, 1, 2)[k], here)), j, 1 - h, -step)

        def finish(self):
            taken(self.some(4), self.in_sem.at[6])

    full, quarter, columns = RHS // 2, RHS // 4, NZ * RANK // 2

    def coeff_piece(h, block, part):
        return coeff_all.at[block, pl.ds(h * full, full) if part is None else pl.ds(h * full + part * quarter, quarter)]

    def top_piece(h, block, part):
        return top_rows.at[h, block] if part is None else top_rows.at[h, block, :, pl.ds(part * columns, columns)]

    of_coeffs = Gather(coeff_piece, lambda n: coeff_all.at[pl.ds(0, n)], send_sem.at[2], c_recv)
    of_top = Gather(top_piece, lambda n: top_rows.at[:, pl.ds(0, n)], send_sem.at[3], w_recv)

    loads["inv"].wait()
    reach = dot(basis[...].T, inv[...]).astype(BF16)
    gather = dot(reach, point[...]).astype(BF16)
    loads["sides"].wait()
    coeff_all[leaf] = dot(gather, sides[...]).T.astype(BF16)

    taken(top_rows.at[0, 0], x_sem.at[0])
    of_top.near()
    of_coeffs.near()
    pl.semaphore_wait(known_sem.at[0], 2)
    signal(known_sem.at[1], along_z(2))
    signal(known_sem.at[1], along_z(-2))

    loads["core"].wait()
    taken(trans_all.at[pl.ds(0, NB - 1)], t_recv.at[0])
    mixed = trans[...] - dot(core[...], trans_all[...].reshape(NB * RANK, RANK))
    part[...] = dot(coeff_all[leaf], mixed.astype(BF16)).astype(BF16).reshape(NB, PART, RANK)
    for to in peers:
        send(part.at[to["ba"]], part_all.at[leaf], send_sem.at[4], r_recv.at[0], to)
    part_all[leaf] = part[leaf]
    pl.semaphore_wait(known_sem.at[1], 2)
    signal(known_sem.at[2], along_z(4))
    signal(known_sem.at[2], along_z(-4))
    of_top.over(0)
    of_top.relay_near()
    of_top.over(1)
    of_top.over(2)

    point_t[...] = (lax.broadcasted_iota(jnp.int32, (LEAF, LEAF), 0) == order[...]).astype(F32).astype(BF16)
    for i in range(2):
        rows = pl.ds(i * 512, 512)
        pinv[rows] = dot(point_t[rows], inv[...]).astype(BF16)
    of_coeffs.relay_near()
    core_t[...] = core[...].T
    pl.semaphore_wait(known_sem.at[2], 2)

    taken(part_all.at[pl.ds(0, NB - 1)], r_recv.at[0])
    total = jnp.sum(part_all[...].astype(F32), axis=0)
    zall[at_z] = total.astype(BF16)
    for d in (NZ // 2, *[d for k in range(NZ // 2 - 1, 0, -1) for d in (k, -k)]):
        send(zall.at[at_z], zall.at[at_z], send_sem.at[5], z_recv.at[0], along_z(d))

    of_top.over(3)
    for k in range(3):
        of_coeffs.over(k)
    for k in range(3):
        of_top.relay_over(k)
    ordered[...] = dot(point[...], sides[...]).astype(BF16)
    of_top.relay_over(3)
    stretch[...] = dot(pinv[...], basis[...]).astype(BF16)
    of_coeffs.over(3)

    for i in range(2):
        rows = pl.ds(i * 512, 512)
        applied[rows] = dot(pinv[rows], ordered[...])
    spread = dot(stretch[...], trans[...].astype(BF16)).astype(BF16)
    for k in range(3):
        of_coeffs.relay_over(k)
    of_top.finish()
    for k in range(2):
        top_rows_t[:, k * RANK : (k + 1) * RANK] = top_rows[k].reshape(RANK, NZ * RANK).T
    taken(zall.at[pl.ds(0, NZ - 1)], z_recv.at[0])
    got = dot(jnp.concatenate([zall[k] for k in range(NZ)], axis=1), top_rows_t[...])
    half[0] = got[:, :RANK]
    half[1] = got[:, RANK:]
    send(half.at[1 - half_id], half_in, send_sem.at[6], x_sem.at[1], partner)
    of_coeffs.relay_over(3)
    taken(half_in, x_sem.at[1])
    slices[leaf] = (half[half_id] + half_in[...]).astype(BF16)
    for to in peers:
        send(slices.at[leaf], slices.at[leaf], send_sem.at[7], s_recv.at[0], to)

    def of_blocks(h, steps):
        blocks = [index(moved(1 - h, step, moved(h, other, here))) for step in steps for other in range(SIDE)]
        left = jnp.concatenate([coeff_all[k, h * full : (h + 1) * full] for k in blocks], axis=1)
        return dot(left, jnp.concatenate([core_t[pl.ds(pl.multiple_of(k * RANK, RANK), RANK)] for k in blocks], axis=0))

    early = [of_blocks(h, (0, 1, -1)) for h in (0, 1)]
    of_coeffs.finish()
    lowered = jnp.concatenate([early[h] + of_blocks(h, (2,)) for h in (0, 1)], axis=0).astype(BF16).T
    for i, ref in enumerate(
        (
            trans_all.at[pl.ds(0, NB - 1)], topsel, coeff_all.at[pl.ds(0, NB - 1)], top_rows.at[:, pl.ds(0, NB - 1)],
            part_all.at[pl.ds(0, NB - 1)], zall.at[pl.ds(0, NZ - 1)], half_in,
        )
    ):
        taken(ref, send_sem.at[i])

    taken(slices.at[pl.ds(0, NB - 1)], s_recv.at[0])
    top = slices[...].reshape(RHS, RANK).T
    both = dot(jnp.concatenate([stretch[...], spread], axis=1), jnp.concatenate([lowered, top], axis=0))
    out[...] = (applied[...] - both).astype(BF16)
    taken(slices.at[pl.ds(0, NB - 1)], send_sem.at[7])


def shards(*args):
    dma = pltpu.SemaphoreType.DMA
    vmem = pltpu.VMEM
    scratch = [
        vmem((LEAF, RHS), BF16), vmem((1, LEAF), jnp.int32), vmem((1, RANK), jnp.int32), vmem((LEAF, LEAF), BF16),
        vmem((LEAF, RANK), BF16), vmem((RANK, NB * RANK), BF16), vmem((RANK, RANK), F32), vmem((8, 2 * NZ * RANK), BF16),
        vmem((LEAF, LEAF), BF16), vmem((LEAF, LEAF), BF16), vmem((LEAF, LEAF), BF16), vmem((LEAF, RHS), BF16),
        vmem((LEAF, RHS), F32), vmem((LEAF, RANK), BF16),
        vmem((NB, RANK, RANK), BF16), vmem((NB, RHS, RANK), BF16), vmem((NB, PART, RANK), BF16), vmem((NB, PART, RANK), BF16),
        vmem((8, NZ * RANK), BF16), vmem((2, NB, 8, NZ * RANK), BF16), vmem((NZ * RANK, 2 * RANK), BF16),
        vmem((NB * RANK, RANK), BF16), vmem((NZ, PART, RANK), BF16), vmem((2, PART, RANK), F32), vmem((PART, RANK), F32),
        vmem((NB, PART, RANK), BF16),
        dma((8,)), dma((8,)), dma((1,)), dma((2,)), dma((7,)), dma((1,)), dma((7,)), dma((1,)), dma((1,)),
        pltpu.SemaphoreType.REGULAR((3,)),
    ]
    return pl.pallas_call(
        kernel,
        out_shape=jax.ShapeDtypeStruct((LEAF, RHS), BF16),
        in_specs=[pl.BlockSpec(memory_space=pl.ANY)] * 8,
        out_specs=pl.BlockSpec(memory_space=pltpu.VMEM),
        scratch_shapes=scratch,
        compiler_params=pltpu.CompilerParams(collective_id=0, has_side_effects=True, vmem_limit_bytes=40 * 2**20),
        name="woodbury",
    )(*[pltpu.with_memory_space_constraint(a, pltpu.HBM) for a in args])


def solution(mesh):
    split = P(("aa", "ba"), None)
    return jax.shard_map(shards, mesh=mesh, in_specs=(split,) * 8, out_specs=split, check_vma=False)
```
